32 devices in a mesh: parts: 1, chan: 16 (over z, y, core), tm: 2 (over x), freq: 1.
Axes of the slice: x: 2, y: 2, z: 4, core: 2. Of those that a mesh axis runs over, the one named last changes fastest.
Arguments:
- spectra: bfloat16 [2, 512, 16, 2048], P(None, 'freq', 'tm', ('parts', 'chan')), may hold values from -6 to 6
- owners: int32 [4], P('parts'), may hold values from 0 to 15
- source_rows: int32 [4, 16], P('parts'), may hold values from 0 to 127
Outputs:
- correlations: float32 [4, 16, 2048, 128], P(None, ('tm', 'freq'), ('parts', 'chan'))
The draws below stay inside these ranges and needn't reach their ends.
All inputs are finite; a program needn't handle non-finite values.
Results may differ from the reference program's by a relative error of at most 0.0037.
Values may be sent and summed in bfloat16 or wider, within the bound.
A program may use at most 64 MiB of HBM per device.

```python
import jax
import jax.numpy as jnp
from jax import lax

FREQ_BINS = 512
WINDOW_LEN = 4096
FIRST_BIN = 64
SOURCES = 16
LAGS = 128
STEPS = 4
C_DEV = 128
CHANNELS = 2048
WINDOWS = 16
SHARDS = 16
N_CHAN = 16


def place_ends(result, key, low, top_value):
    spot = [jax.random.randint(jax.random.fold_in(key, axis), (), 0, length) for axis, length in enumerate(result.shape)]
    main_axis = result.shape.index(max(result.shape))
    next_to = spot[:main_axis] + [(spot[main_axis] + 1) % result.shape[main_axis]] + spot[main_axis + 1:]
    return result.at[tuple(spot)].set(low).at[tuple(next_to)].set(top_value)


def shard_levels(own_key, dims, pieces, smallest, top_value):
    def one(position, parts):
        steps = jax.random.uniform(jax.random.fold_in(jax.random.fold_in(own_key, 6), position), (parts,), jnp.float32, smallest / len(pieces), top_value / len(pieces))
        return jnp.repeat(jnp.exp(steps), dims[position] // parts).reshape((-1,) + (1,) * (len(dims) - position - 1))

    factor_of = one(*pieces[0])
    for cut in pieces[1:]:
        factor_of = factor_of * one(*cut)
    return factor_of


def gaussian(key, extent, width, reach, shards=(), held_as=jnp.bfloat16):
    loudness = shard_levels(key, extent, shards, -0.22, 0.18) if shards else 1.0
    drawn = jax.random.normal(key, extent, jnp.float32) * width * loudness
    return jnp.minimum(jnp.maximum(drawn, -reach), reach).astype(held_as)


def setup_inputs(seed: int = 0, part: int = 0) -> dict:
    streams_of = jax.random.split(jax.random.key(seed), 4)
    part_splits = jax.random.split(jax.random.fold_in(streams_of[3], part), 4)
    return {
        "spectra": gaussian(part_splits[0], (2, FREQ_BINS, WINDOWS, CHANNELS), 1.0, 6.0, ((2, 2), (3, 16))),
        "owners": place_ends(jax.random.randint(part_splits[1], (STEPS,), 0, SHARDS), jax.random.fold_in(part_splits[1], 1), 0, SHARDS - 1).astype(jnp.int32),
        "source_rows": place_ends(jax.random.randint(part_splits[2], (STEPS, SOURCES), 0, C_DEV), jax.random.fold_in(part_splits[2], 1), 0, C_DEV - 1).astype(jnp.int32),
    }


WATER = 0.5

def whiten(block):
    values = block.astype(jnp.float32)
    size = jnp.sqrt(values[0] * values[0] + values[1] * values[1]) + WATER
    return (values / size[None]).astype(jnp.bfloat16)

def make_tables(first_bin, count):
    bins = first_bin + jnp.arange(count, dtype=jnp.int32)
    shifts = jnp.arange(LAGS, dtype=jnp.int32) - LAGS // 2
    phase = jnp.mod(bins[:, None] * shifts[None, :], WINDOW_LEN).astype(jnp.float32)
    angle = phase * (2.0 * 3.141592653589793 / WINDOW_LEN)
    return (jnp.cos(angle), jnp.sin(angle))

def reference(spectra, owners, source_rows):
    chosen = (owners[:, None] * C_DEV + source_rows).reshape(-1).astype(jnp.int32)
    picked = whiten(jnp.take(spectra, chosen, axis=3))
    picked = picked.reshape(2, FREQ_BINS, WINDOWS, STEPS, SOURCES).astype(jnp.float32)
    picked = jnp.transpose(picked, (3, 0, 1, 2, 4))
    flipped = jnp.stack([picked, jnp.stack([-picked[:, 1], picked[:, 0]], axis=1)], axis=1)
    cosine, sine = make_tables(FIRST_BIN, FREQ_BINS)
    hp = lax.Precision.HIGHEST

    def shard_lags(index):
        start = (index * C_DEV).astype(jnp.int32)
        local = lax.dynamic_slice_in_dim(spectra, start, C_DEV, 3)
        local = whiten(local).astype(jnp.float32)
        cross = jnp.einsum('tokfws,kfwc->tofsc', flipped, local, precision=hp)
        lags = jnp.einsum('tfsc,fl->tscl', cross[:, 0], cosine, precision=hp)
        lags = lags - jnp.einsum('tfsc,fl->tscl', cross[:, 1], sine, precision=hp)
        return lags / WINDOWS
    every = lax.map(shard_lags, jnp.arange(N_CHAN, dtype=jnp.int32))
    every = jnp.transpose(every, (1, 2, 0, 3, 4))
    return every.reshape(STEPS, SOURCES, CHANNELS, LAGS)
```

```python
import functools

import jax
import jax.numpy as jnp
import numpy as np
from jax import lax
from jax.experimental import pallas as pl
from jax.experimental.pallas import tpu as pltpu
from jax.sharding import PartitionSpec as P

WINDOW_LEN = 4096
FIRST_BIN = 64
LAGS = 128
WATER = 0.5
AXES = ("parts", "chan", "tm", "freq")
MESH = pl.DeviceIdType.MESH
COMM = True
XCH = True
MUL = True
LAG = True
PREP = True
CLOSE = True
UNROLL = 4


def table(count, scale):
    bins = FIRST_BIN + np.arange(count)
    shifts = np.arange(LAGS) - LAGS // 2
    angle = np.mod(shifts[:, None] * bins[None, :], WINDOW_LEN) * (2.0 * np.pi / WINDOW_LEN)
    return np.concatenate([np.cos(angle), -np.sin(angle)], axis=1) * scale


def factors(count, scale):
    full = table(count, 1.0)
    basis, sizes, _ = np.linalg.svd(full, full_matrices=False)
    rank = 16
    while rank < LAGS and np.sum(sizes[rank:] ** 2) > 1e-22 * np.sum(sizes ** 2):
        rank += 16
    basis = basis[:, :rank]
    return basis, (basis.T @ full).reshape(rank, 2, count) * scale


def kernel(sizes, owner_ref, row_ref, spec_hbm, table_ref, out_ref,
           spec_ref, pick, right, held, got1, got2, got_full, whole, cross, send, recv,
           lsem, bsend, brecv, xsend, xrecv):
    steps, per_step, bins, wins, chans, n_chan, n_tm, n_freq, size, rank_of = sizes
    peers = n_tm * n_freq
    per = per_step // peers
    block = steps * per
    total = steps * per_step
    chunks = total // size
    sends = (peers - 1) * block // size
    some = 64 // wins
    pairs = bins // (2 * some)
    quarter = pairs // 4
    part, me = lax.axis_index("parts"), lax.axis_index("chan")
    tm, fq = lax.axis_index("tm"), lax.axis_index("freq")
    rank = tm * n_freq + fq
    bit0, bit1 = me % 2, (me // 2) % 2
    dists = []
    while 2 ** len(dists) < n_chan:
        dists.append(2 ** len(dists))
    far = dists[2:]
    stages = [1, 2] + far + [2, 1]
    last = len(stages) - 1
    count = len(stages)

    def along(d):
        return (part, me + d * (1 - 2 * ((me // d) % 2)), tm, fq)

    def peer(p):
        other = (rank + p) % peers
        return (part, me, other // n_freq, other % n_freq)

    barrier = pltpu.get_barrier_semaphore()
    for d in dists:
        pl.semaphore_signal(barrier, inc=1, device_id=along(d), device_id_type=MESH)
    for p in range(1, peers):
        pl.semaphore_signal(barrier, inc=1, device_id=peer(p), device_id_type=MESH)

    rows = 64 * pairs
    loads = 4

    def load(n):
        at = pl.ds(n * (rows // loads), rows // loads)
        return [pltpu.make_async_copy(spec_hbm.at[k, h, at], spec_ref.at[k, h, at], lsem.at[2 * (2 * n + h) + k])
                for h in range(2) for k in range(2)]

    for n in range(loads):
        for one in load(n):
            one.start()

    channel = lax.broadcasted_iota(jnp.int32, (1, chans), 1)
    for p in range(1, peers + 1):
        for t in range(steps):
            held_here = owner_ref[t] == me
            for j in range(per):
                row = jnp.where(held_here, row_ref[t, ((rank + p) % peers) * per + j], -1)
                at = (p - 1) * block + t * per + j
                pick[pl.ds(at, 1), :] = (channel == row).astype(jnp.float32)
    chosen = pick[...].astype(jnp.bfloat16)

    def prepare(q, i):
        both = []
        for h in range(2):
            at = pl.ds(pl.multiple_of((q * quarter + i) * 64, 64), 64)
            re = spec_ref[0, h, at, :].astype(jnp.float32)
            im = spec_ref[1, h, at, :].astype(jnp.float32)
            inverse = 1.0 / (jnp.sqrt(re * re + im * im) + WATER)
            re = (re * inverse).astype(jnp.bfloat16)
            im = (im * inverse).astype(jnp.bfloat16)
            g = q * quarter + i
            right[g, h, :64, :chans] = re
            right[g, h, :64, chans:] = im
            right[g, h, 64:, :chans] = im
            right[g, h, 64:, chans:] = -re
            both += [re, im]
        got = lax.dot_general(chosen, jnp.concatenate(both, axis=0), (((1,), (1,)), ((), ())),
                              preferred_element_type=jnp.float32)
        to = pl.ds(pl.multiple_of(i * 128, 128), 128)
        for c in range(chunks):
            mine = got[c * size:(c + 1) * size]
            held[c, q, :, to] = jnp.concatenate([mine[:, :128], mine[:, 128:]], axis=0).astype(jnp.bfloat16)

    def repeat(count, unroll, body):
        unroll = min(unroll, count)

        def some(i, carry):
            for r in range(unroll):
                body(i * unroll + r)
            return carry

        lax.fori_loop(0, count // unroll, some, 0)

    for q in range(4):
        for one in load(q):
            one.wait()
        if PREP:
            repeat(quarter, 2, functools.partial(prepare, q))

    pl.semaphore_wait(barrier, len(dists) + peers - 1)

    keep = 2 * bit0 + bit1

    def copy(t, st):
        d = stages[st]
        if st == 0:
            src, dst = held.at[t, pl.ds(2 * (1 - bit0), 2)], got1.at[t]
        elif st == 1:
            src, dst = held.at[t, 2 * bit0 + 1 - bit1], got2.at[t]
        elif st < last - 1:
            src, dst = held.at[t, keep], got_full.at[t, st - 2]
        elif st == last - 1:
            src = dst = whole.at[t, keep]
        else:
            src = dst = whole.at[t, pl.ds(2 * bit0, 2)]
        return pltpu.make_async_remote_copy(
            src_ref=src, dst_ref=dst, send_sem=bsend.at[t, st], recv_sem=brecv.at[t, st],
            device_id=along(d), device_id_type=MESH)

    def finish(t, st):
        if COMM:
            copy(t, st).wait()
        if st == 0:
            for q in range(2):
                held[t, 2 * bit0 + q] = held[t, 2 * bit0 + q] + got1[t, q]
        elif st == 1:
            held[t, keep] = held[t, keep] + got2[t]
        elif st < last - 1:
            held[t, keep] = held[t, keep] + got_full[t, st - 2]
        if st == last - 2:
            whole[t, keep] = held[t, keep]
        if st + 1 < count and COMM:
            copy(t, st + 1).start()

    lane = lax.broadcasted_iota(jnp.int32, (1, some, 128), 2)
    bin_of = lax.broadcasted_iota(jnp.int32, (1, some, 128), 1)
    mine = ((lane % 64) // wins) == bin_of

    def exchange(v):
        return pltpu.make_async_remote_copy(
            src_ref=send.at[v], dst_ref=recv.at[v], send_sem=xsend.at[v], recv_sem=xrecv.at[v],
            device_id=peer(v * size // block + 1), device_id_type=MESH)

    def multiply(u, q):
        def one(i):
            x = whole[u, q, :, pl.ds(pl.multiple_of(i * 128, 128), 128)].astype(jnp.float32)
            g = q * quarter + i
            got = []
            for h in range(2):
                wide = jnp.where(mine, x[h * size:(h + 1) * size, None, :], 0.0)
                left = wide.reshape(size * some, 128).astype(jnp.bfloat16)
                got.append(jnp.dot(left, right[g, h], preferred_element_type=jnp.float32).reshape(size, some, 2 * chans))
            for o in range(2):
                to = pl.ds(pl.multiple_of(o * bins + g * 2 * some, 2 * some), 2 * some)
                value = jnp.concatenate([got[h][:, :, o * chans:(o + 1) * chans] for h in range(2)], axis=1)
                cross[:, to, :] = value.astype(jnp.bfloat16)

        if MUL:
            repeat(quarter, UNROLL, one)

    def lag(v, i):
        both = jnp.concatenate([cross[2 * i], cross[2 * i + 1]], axis=1)
        got = jnp.dot(table_ref[...], both, preferred_element_type=jnp.float32)
        for r in range(2):
            value = got[:, r * chans:(r + 1) * chans]
            if v < sends:
                send[v, 2 * i + r] = value.astype(jnp.bfloat16)
            else:
                out_ref[(v - sends) * size + 2 * i + r] = value

    def lags(v):
        if LAG:
            repeat(size // 2, 2, functools.partial(lag, v))
        if v < sends and XCH:
            exchange(v).start()

    def close(w):
        for p in range(1, peers):
            v = (p - 1) * (block // size) + w
            if XCH:
                exchange(v).wait()
            for j in range(size):
                out_ref[w * size + j] = out_ref[w * size + j] + recv[v, j].astype(jnp.float32)

    for t in range(chunks):
        if COMM:
            copy(t, 0).start()
    for wave in range(chunks + count):
        events = [functools.partial(finish, t, wave - t) for t in range(chunks) if 0 <= wave - t < count]
        work = []
        u = wave - count
        if 0 <= u < chunks:
            work = [functools.partial(multiply, u, q) for q in range(4)] + [functools.partial(lags, u)]
        line = [((n + 0.5) / len(events), n, e) for n, e in enumerate(events)]
        line += [((n + 0.6) / len(work), n + 100, e) for n, e in enumerate(work)]
        for _, _, act in sorted(line, key=lambda a: a[:2]):
            act()
    for w in range(block // size):
        if CLOSE:
            close(w)


def expand(coef_ref, basis_ref, out_ref):
    for j in range(coef_ref.shape[0]):
        value = coef_ref[j]
        high = value.astype(jnp.bfloat16)
        low = (value - high.astype(jnp.float32)).astype(jnp.bfloat16)
        both = jnp.concatenate([high, high, low], axis=0)
        out_ref[j] = lax.dot_general(both, basis_ref[...], (((0,), (0,)), ((), ())),
                                     preferred_element_type=jnp.float32)


def per_device(spectra, owners, source_rows):
    _, bins, wins, chans = spectra.shape
    steps, per_step = source_rows.shape
    n_chan, n_tm, n_freq = (lax.axis_size(a) for a in AXES[1:])
    peers = n_tm * n_freq
    per = per_step // peers
    block = steps * per
    size = min(8, block)
    chunks = steps * per_step // size
    some = 64 // wins
    pairs = bins // (2 * some)
    basis, rest = factors(bins * n_freq, 1.0 / (wins * n_tm))
    rank = basis.shape[1]
    rest = rest.reshape(rank, 2, n_freq, 2, pairs, some).transpose(2, 0, 1, 4, 3, 5).reshape(n_freq, rank, 2 * bins)
    rest = jnp.asarray(rest.astype(jnp.bfloat16))
    rest = lax.dynamic_index_in_dim(rest, lax.axis_index("freq"), 0, False) if n_freq > 1 else rest[0]
    high = basis.T.astype(np.float32).astype(jnp.bfloat16)
    low = (basis.T - high.astype(np.float64)).astype(jnp.bfloat16)
    spread = jnp.asarray(np.concatenate([high, low, high], axis=0))
    far = max(n_chan.bit_length() - 3, 1)
    count = n_chan.bit_length() + 1
    sizes = (steps, per_step, bins, wins, chans, n_chan, n_tm, n_freq, size, rank)
    bf16, f32 = jnp.bfloat16, jnp.float32
    quarter = (2 * size, pairs // 4 * 128)
    vmem = pl.BlockSpec(memory_space=pltpu.VMEM)
    smem = pl.BlockSpec(memory_space=pltpu.SMEM)
    sends = max((peers - 1) * block // size, 1)
    coef = pl.pallas_call(
        functools.partial(kernel, sizes),
        out_shape=jax.ShapeDtypeStruct((block, rank, chans), f32),
        in_specs=[smem, smem, pl.BlockSpec(memory_space=pl.ANY), vmem],
        out_specs=vmem,
        scratch_shapes=[
            pltpu.VMEM((2, 2, bins * wins // 2, chans), bf16),
            pltpu.VMEM((steps * per_step, chans), f32),
            pltpu.VMEM((pairs, 2, 128, 2 * chans), bf16),
            pltpu.VMEM((chunks, 4) + quarter, bf16),
            pltpu.VMEM((chunks, 2) + quarter, bf16),
            pltpu.VMEM((chunks,) + quarter, bf16),
            pltpu.VMEM((chunks, far) + quarter, bf16),
            pltpu.VMEM((chunks, 4) + quarter, bf16),
            pltpu.VMEM((size, 2 * bins, chans), bf16),
            pltpu.VMEM((sends, size, rank, chans), bf16),
            pltpu.VMEM((sends, size, rank, chans), bf16),
            pltpu.SemaphoreType.DMA((16,)),
            pltpu.SemaphoreType.DMA((chunks, count)),
            pltpu.SemaphoreType.DMA((chunks, count)),
            pltpu.SemaphoreType.DMA((sends,)),
            pltpu.SemaphoreType.DMA((sends,)),
        ],
        compiler_params=pltpu.CompilerParams(collective_id=0, has_side_effects=True),
    )(owners, source_rows, spectra.reshape(2, 2, bins * wins // 2, chans), rest)
    tile = min(8, block)
    out = pl.pallas_call(
        expand,
        out_shape=jax.ShapeDtypeStruct((block, chans, LAGS), f32),
        grid=(block // tile,),
        in_specs=[pl.BlockSpec((tile, rank, chans), lambda i: (i, 0, 0)),
                  pl.BlockSpec((3 * rank, LAGS), lambda i: (0, 0))],
        out_specs=pl.BlockSpec((tile, chans, LAGS), lambda i: (i, 0, 0)),
    )(coef, spread)
    return out.reshape(steps, per, chans, LAGS)


def solution(mesh):
    placed = (P(None, "freq", "tm", ("parts", "chan")), P("parts"), P("parts", None))
    return jax.shard_map(
        per_device,
        mesh=mesh,
        in_specs=placed,
        out_specs=P(None, ("tm", "freq"), ("parts", "chan"), None),
        check_vma=False,
    )
```

```python
import functools

import jax
import jax.numpy as jnp
import numpy as np
from jax import lax
from jax.experimental import pallas as pl
from jax.experimental.pallas import tpu as pltpu
from jax.sharding import PartitionSpec as P

WINDOW_LEN = 4096
FIRST_BIN = 64
LAGS = 128
WATER = 0.5
AXES = ("parts", "chan", "tm", "freq")
MESH = pl.DeviceIdType.MESH
COMM = True
XCH = True
MUL = True
LAG = True
PREP = 1
DEPTH = 4
PUNROLL = 4
CLOSE = True
UNROLL = 32
DIRECT = 4
GAP = 1.8
SHIFT = 0.0
RED = 5.2
GAT = 10.0
BT = (5.3, 10.6, 14.5, 17.7, 18.7, 18.75)
VLIM = None
TILES = 2


def table(count, scale):
    bins = FIRST_BIN + np.arange(count)
    shifts = np.arange(LAGS) - LAGS // 2
    angle = np.mod(shifts[:, None] * bins[None, :], WINDOW_LEN) * (2.0 * np.pi / WINDOW_LEN)
    return np.concatenate([np.cos(angle), -np.sin(angle)], axis=1) * scale


def factors(count, scale):
    full = table(count, 1.0)
    basis, sizes, _ = np.linalg.svd(full, full_matrices=False)
    rank = 8
    while rank < LAGS and np.sum(sizes[rank:] ** 2) > 1e-20 * np.sum(sizes ** 2):
        rank += 8
    basis = basis[:, :rank]
    return basis, (basis.T @ full).reshape(rank, 2, count) * scale


def group_of(n_chan):
    return max(min(8, n_chan // 2), 1)


def kernel(sizes, owner_hbm, row_hbm, spec_hbm, table_hbm, out_ref,
           owner_ref, row_ref, table_ref, spec_ref, pick, right, held, got1, got2, got_far, whole, cross, send, recv,
           lsem, csend, crecv, gsend, grecv, fsend, frecv, asend, arecv, xsend, xrecv):
    steps, per_step, bins, wins, chans, n_chan, n_tm, n_freq, size, rank_of = sizes
    peers = n_tm * n_freq
    per = per_step // peers
    block = steps * per
    total = steps * per_step
    chunks = total // size
    sends = (peers - 1) * block // size
    some = 64 // wins
    pairs = bins // (2 * some)
    group = group_of(n_chan)
    each = pairs // (2 * group)
    part, me = lax.axis_index("parts"), lax.axis_index("chan")
    tm, fq = lax.axis_index("tm"), lax.axis_index("freq")
    rank = tm * n_freq + fq
    half = me % 2
    spot = (me // 2) % group
    quads = max(group // 2, 1)
    side, deep = spot % 2, spot // 2
    slot = side * quads + deep if group > 1 else 0
    far = []
    while 2 * group * 2 ** len(far) < n_chan:
        far.append(2 * group * 2 ** len(far))

    def along(mask):
        other, d = me, 1
        while d <= mask:
            if mask & d:
                other = other + d * (1 - 2 * ((me // d) % 2))
            d *= 2
        return other

    def chan(mask):
        return (part, along(mask), tm, fq)

    def peer(p):
        other = (rank + p) % peers
        return (part, me, other // n_freq, other % n_freq)

    barrier = pltpu.get_barrier_semaphore()
    near = [1] + [2 * k for k in range(1, group)] + far
    for d in near:
        pl.semaphore_signal(barrier, inc=1, device_id=chan(d), device_id_type=MESH)
    for p in range(1, peers):
        pl.semaphore_signal(barrier, inc=1, device_id=peer(p), device_id_type=MESH)

    rows = 64 * pairs
    loads = 4

    def load(n):
        at = pl.ds(n * (rows // loads), rows // loads)
        return [pltpu.make_async_copy(spec_hbm.at[k, h, at], spec_ref.at[k, h, at], lsem.at[2 * (2 * n + h) + k])
                for h in range(2) for k in range(2)]

    small = [pltpu.make_async_copy(src, dst, lsem.at[16 + n]) for n, (src, dst) in enumerate(
        [(owner_hbm, owner_ref), (row_hbm, row_ref), (table_hbm, table_ref)])]
    for one in small[:2]:
        one.start()
    for n in range(loads):
        for one in load(n):
            one.start()
    small[2].start()
    for one in small:
        one.wait()

    channel = lax.broadcasted_iota(jnp.int32, (1, chans), 1)
    for p in range(1, peers + 1):
        for t in range(steps):
            held_here = owner_ref[t] == me
            for j in range(per):
                row = jnp.where(held_here, row_ref[t, ((rank + p) % peers) * per + j], -1)
                at = (p - 1) * block + t * per + j
                pick[pl.ds(at, 1), :] = (channel == row).astype(jnp.float32)
    chosen = pick[...].astype(jnp.bfloat16)

    def prepare(i):
        both = []
        for h in range(2):
            at = pl.ds(pl.multiple_of(i * 64, 64), 64)
            re = spec_ref[0, h, at, :].astype(jnp.float32)
            im = spec_ref[1, h, at, :].astype(jnp.float32)
            inverse = 1.0 / (jnp.sqrt(re * re + im * im) + WATER)
            re = (re * inverse).astype(jnp.bfloat16)
            im = (im * inverse).astype(jnp.bfloat16)
            right[i, h, :64, :chans] = re
            right[i, h, :64, chans:] = im
            right[i, h, 64:, :chans] = im
            right[i, h, 64:, chans:] = -re
            both += [re, im]
        got = lax.dot_general(chosen, jnp.concatenate(both, axis=0), (((1,), (1,)), ((), ())),
                              preferred_element_type=jnp.float32)
        for c in range(chunks):
            mine = got[c * size:(c + 1) * size]
            mine = jnp.concatenate([mine[:, :128], mine[:, 128:]], axis=0).astype(jnp.bfloat16)
            held[c, i // (pairs // 2), (i // each) % group, i % each] = mine

    def repeat(first, count, unroll, body):
        unroll = min(unroll, count)

        def some(i, carry):
            for r in range(unroll):
                body(first + i * unroll + r)
            return carry

        lax.fori_loop(0, count // unroll, some, 0)

    for n in range(loads):
        for one in load(n):
            one.wait()
        for _ in range(PREP):
            repeat(n * (pairs // loads), pairs // loads, PUNROLL, prepare)

    pl.semaphore_wait(barrier, len(near) + peers - 1)

    def core(c, back):
        if back:
            src = dst = whole.at[c, half]
        else:
            src, dst = held.at[c, 1 - half], got1.at[c]
        return pltpu.make_async_remote_copy(
            src_ref=src, dst_ref=dst, send_sem=csend.at[c, back], recv_sem=crecv.at[c, back],
            device_id=chan(1), device_id_type=MESH)

    def send_to(mask, c, n, src, dst, pair):
        return pltpu.make_async_remote_copy(
            src_ref=src, dst_ref=dst, send_sem=pair[0].at[c, n], recv_sem=pair[1].at[c, n],
            device_id=chan(mask), device_id_type=MESH)

    def place(k):
        other = (along(2 * k) // 2) % group
        return (other % 2) * quads + other // 2

    def scatter(c, k):
        return send_to(2 * k, c, k - 1, held.at[c, half, place(k)], got2.at[c, k - 1], (gsend, grecv))

    def gather(c, k):
        return send_to(2 * k, c, k - 1, whole.at[c, half, slot], whole.at[c, half, slot], (asend, arecv))

    def scatter_side(c):
        return send_to(2, c, 0, held.at[c, half, pl.ds((1 - side) * quads, quads)], got2.at[c, pl.ds(0, quads)],
                       (gsend, grecv))

    def gather_side(c):
        at = pl.ds(side * quads, quads)
        return send_to(2, c, 0, whole.at[c, half, at], whole.at[c, half, at], (asend, arecv))

    def scatter_deep(c, k):
        n = quads + k - 1
        return send_to(4 * k, c, n, held.at[c, half, place(2 * k)], got2.at[c, n], (gsend, grecv))

    def gather_deep(c, k):
        return send_to(4 * k, c, quads + k - 1, whole.at[c, half, slot], whole.at[c, half, slot], (asend, arecv))

    def double(c, n):
        return send_to(far[n], c, n, held.at[c, half, slot], got_far.at[c, n], (fsend, frecv))

    def start(copies):
        if COMM:
            for one in copies:
                one.start()

    def wait(copies):
        if COMM:
            for one in copies:
                one.wait()

    def several(make, c, count):
        return [make(c, k) for k in range(count - 1, 0, -1)]

    def summed(c, value, make, count, base):
        for k in range(1, count):
            wait([make(c, k)])
            value = value + got2[c, base + k - 1]
        for n in range(len(far)):
            held[c, half, slot] = value
            start([double(c, n)])
            wait([double(c, n)])
            value = value + got_far[c, n]
        whole[c, half, slot] = value

    def joined(c):
        wait([core(c, 0)])
        held[c, half] = held[c, half] + got1[c]
        if c in direct:
            start(several(scatter, c, group))
        else:
            start([scatter_side(c)])

    def sided(c):
        wait([scatter_side(c)])
        at = pl.ds(side * quads, quads)
        held[c, half, at] = held[c, half, at] + got2[c, :quads]
        start(several(scatter_deep, c, quads))

    def reduced(c):
        if c in direct:
            summed(c, held[c, half, slot], scatter, group, 0)
            start(several(gather, c, group))
        else:
            summed(c, held[c, half, slot], scatter_deep, quads, quads)
            start(several(gather_deep, c, quads))

    def deepened(c):
        wait(several(gather_deep, c, quads))
        start([gather_side(c)])

    def gathered(c):
        wait(several(gather, c, group) if c in direct else [gather_side(c)])
        start([core(c, 1)])

    def arrived(c):
        wait([core(c, 1)])

    direct = range(chunks if group < 2 else min(DIRECT, chunks))

    lane = lax.broadcasted_iota(jnp.int32, (1, some, 128), 2)
    bin_of = lax.broadcasted_iota(jnp.int32, (1, some, 128), 1)
    mine = ((lane % 64) // wins) == bin_of

    def exchange(v):
        return pltpu.make_async_remote_copy(
            src_ref=send.at[v], dst_ref=recv.at[v], send_sem=xsend.at[v], recv_sem=xrecv.at[v],
            device_id=peer(v * size // block + 1), device_id_type=MESH)

    def multiply(u):
        def one(g):
            x = whole[u, g // (pairs // 2), (g // each) % group, g % each].astype(jnp.float32)
            got = []
            for h in range(2):
                wide = jnp.where(mine, x[h * size:(h + 1) * size, None, :], 0.0)
                left = wide.reshape(size * some, 128).astype(jnp.bfloat16)
                got.append(jnp.dot(left, right[g, h], preferred_element_type=jnp.float32).reshape(size, some, 2 * chans))
            for o in range(2):
                to = pl.ds(o * bins + g * 2 * some, 2 * some)
                value = jnp.concatenate([got[h][:, :, o * chans:(o + 1) * chans] for h in range(2)], axis=1)
                cross[:, to, :] = value.astype(jnp.bfloat16)

        if MUL:
            repeat(0, pairs, UNROLL, one)

    def lag(v, i):
        both = jnp.concatenate([cross[2 * i], cross[2 * i + 1]], axis=1)
        got = jnp.dot(table_ref[...], both, preferred_element_type=jnp.float32)
        if v < sends:
            both = jnp.concatenate([got[:, :chans], got[:, chans:]], axis=0)
            send[v, 2 * i * rank_of:2 * (i + 1) * rank_of] = both.astype(jnp.bfloat16)
        else:
            for r in range(2):
                out_ref[(v - sends) * size + 2 * i + r] = got[:, r * chans:(r + 1) * chans]

    def compute(v):
        multiply(v)
        if LAG:
            for i in range(size // 2):
                lag(v, i)
        if v < sends and XCH:
            exchange(v).start()

    def close(w):
        for p in range(1, peers):
            v = (p - 1) * (block // size) + w
            if XCH:
                exchange(v).wait()
            for j in range(0, size, 2):
                value = recv[v, j * rank_of:(j + 2) * rank_of].astype(jnp.float32)
                for r in range(2):
                    at = w * size + j + r
                    out_ref[at] = out_ref[at] + value[r * rank_of:(r + 1) * rank_of]

    order = []
    for c in range(chunks):
        order.append((0.01 * c, joined, c))
        if c in direct:
            lag_of = GAP * c
            times = [(RED, reduced), (GAT, gathered), (GAT + 0.9, arrived), (GAT + 0.95, compute)]
        else:
            lag_of = GAP * (c - len(direct)) + SHIFT
            times = list(zip(BT, (sided, reduced, deepened, gathered, arrived, compute)))
        order += [(at + lag_of, act, c) for at, act in times]
    for c in range(chunks):
        start([core(c, 0)])
    for _, act, c in sorted(order, key=lambda a: (a[0], a[2])):
        act(c)
    for w in range(block // size):
        if CLOSE:
            close(w)


def expand(coef_ref, basis_ref, out_ref):
    for j in range(coef_ref.shape[0]):
        value = coef_ref[j]
        high = value.astype(jnp.bfloat16)
        low = (value - high.astype(jnp.float32)).astype(jnp.bfloat16)
        both = jnp.concatenate([high, high, low], axis=0)
        out_ref[j] = lax.dot_general(both, basis_ref[...], (((0,), (0,)), ((), ())),
                                     preferred_element_type=jnp.float32)


def per_device(spectra, owners, source_rows):
    _, bins, wins, chans = spectra.shape
    steps, per_step = source_rows.shape
    n_chan, n_tm, n_freq = (lax.axis_size(a) for a in AXES[1:])
    peers = n_tm * n_freq
    per = per_step // peers
    block = steps * per
    size = min(8, block)
    chunks = steps * per_step // size
    some = 64 // wins
    pairs = bins // (2 * some)
    basis, rest = factors(bins * n_freq, 1.0 / (wins * n_tm))
    rank = basis.shape[1]
    rest = rest.reshape(rank, 2, n_freq, 2, pairs, some).transpose(2, 0, 1, 4, 3, 5).reshape(n_freq, rank, 2 * bins)
    rest = jnp.asarray(rest.astype(jnp.bfloat16))
    rest = lax.dynamic_index_in_dim(rest, lax.axis_index("freq"), 0, False) if n_freq > 1 else rest[0]
    high = basis.T.astype(np.float32).astype(jnp.bfloat16)
    low = (basis.T - high.astype(np.float64)).astype(jnp.bfloat16)
    spread = jnp.asarray(np.concatenate([high, low, high], axis=0))
    group = group_of(n_chan)
    far = max((n_chan // (2 * group)).bit_length() - 1, 1)
    sizes = (steps, per_step, bins, wins, chans, n_chan, n_tm, n_freq, size, rank)
    bf16, f32 = jnp.bfloat16, jnp.float32
    piece = (pairs // (2 * group), 2 * size, 128)
    vmem = pl.BlockSpec(memory_space=pltpu.VMEM)
    sends = max((peers - 1) * block // size, 1)
    links = max(group - 1, 1)
    dma = pltpu.SemaphoreType.DMA
    coef = pl.pallas_call(
        functools.partial(kernel, sizes),
        out_shape=jax.ShapeDtypeStruct((block, rank, chans), f32),
        in_specs=[pl.BlockSpec(memory_space=pl.ANY)] * 4,
        out_specs=vmem,
        scratch_shapes=[
            pltpu.SMEM((steps,), jnp.int32),
            pltpu.SMEM((steps, per_step), jnp.int32),
            pltpu.VMEM((rank, 2 * bins), bf16),
            pltpu.VMEM((2, 2, bins * wins // 2, chans), bf16),
            pltpu.VMEM((steps * per_step, chans), f32),
            pltpu.VMEM((pairs, 2, 128, 2 * chans), bf16),
            pltpu.VMEM((chunks, 2, group) + piece, bf16),
            pltpu.VMEM((chunks, group) + piece, bf16),
            pltpu.VMEM((chunks, links) + piece, bf16),
            pltpu.VMEM((chunks, far) + piece, bf16),
            pltpu.VMEM((chunks, 2, group) + piece, bf16),
            pltpu.VMEM((size, 2 * bins, chans), bf16),
            pltpu.VMEM((sends, size * rank, chans), bf16),
            pltpu.VMEM((sends, size * rank, chans), bf16),
            dma((19,)), dma((chunks, 2)), dma((chunks, 2)), dma((chunks, links)), dma((chunks, links)),
            dma((chunks, far)), dma((chunks, far)), dma((chunks, links)), dma((chunks, links)),
            dma((sends,)), dma((sends,)),
        ],
        compiler_params=pltpu.CompilerParams(collective_id=0, has_side_effects=True, vmem_limit_bytes=VLIM),
    )(owners, source_rows, spectra.reshape(2, 2, bins * wins // 2, chans), rest)
    tile = block // TILES
    out = pl.pallas_call(
        expand,
        out_shape=jax.ShapeDtypeStruct((block, chans, LAGS), f32),
        grid=(block // tile,),
        in_specs=[pl.BlockSpec((tile, rank, chans), lambda i: (i, 0, 0)),
                  pl.BlockSpec((3 * rank, LAGS), lambda i: (0, 0))],
        out_specs=pl.BlockSpec((tile, chans, LAGS), lambda i: (i, 0, 0)),
    )(coef, spread)
    return out.reshape(steps, per, chans, LAGS)


def solution(mesh):
    placed = (P(None, "freq", "tm", ("parts", "chan")), P("parts"), P("parts", None))
    return jax.shard_map(
        per_device,
        mesh=mesh,
        in_specs=placed,
        out_specs=P(None, ("tm", "freq"), ("parts", "chan"), None),
        check_vma=False,
    )
```

```python
import functools

import jax
import jax.numpy as jnp
import numpy as np
from jax import lax
from jax.experimental import pallas as pl
from jax.experimental.pallas import tpu as pltpu
from jax.sharding import PartitionSpec as P

WINDOW_LEN = 4096
FIRST_BIN = 64
LAGS = 128
WATER = 0.5
AXES = ("parts", "chan", "tm", "freq")
MESH = pl.DeviceIdType.MESH
COMM = True
XCH = True
MUL = True
LAG = True
CLOSE = True
KINDS = "WWWNNNNN"
UNROLL = 32
WAYS = {
    "W": (("core", 1.0, (0.1, 0, 0, 0)), ("scatter", 2.9, (0, 0.6, 0.9, 1.5)), ("gather", 2.9, (0, 0.6, 0.9, 1.5)),
          ("back", 1.0, (0.1, 0, 0, 0))),
    "N": (("core", 1.0, (0.1, 0, 0, 0)), ("side", 2.1, (0, 0.6, 0, 0)), ("near", 2.1, (0, 0, 0.6, 0)),
          ("next", 2.5, (0, 0, 0.6, 1.2)), ("gather", 2.1, (0, 0.6, 0, 0)), ("back", 1.0, (0.1, 0, 0, 0))),
}
COST = {"core": 0.2, "scatter": 0.35, "side": 0.15, "near": 0.15, "next": 0.15, "gather": 0.1, "back": 0.05}
WORK, LAST, CROSS, REACH = 1.05, 0.15, 2.15, 2.2


def schedule(chunks, sends, kinds, halvings):
    ways = []
    for c in range(chunks):
        way = WAYS[kinds[c]]
        ways.append([one for one in way if one[0] not in ("near", "next")[halvings:]])
    free, cross, now = [0.0] * 4, 0.0, 0.0
    due, line, ready, kept, landed = {}, [], [], [], {}

    def send(c, stage):
        _, wait, loads = ways[c][stage]
        end = now
        for n, load in enumerate(loads):
            if load:
                free[n] = max(now, free[n]) + load
                end = max(end, free[n])
        due[c] = (stage, end + wait)

    for c in range(chunks):
        send(c, 0)
    while due or ready:
        done = [c for c in sorted(due) if due[c][1] <= now]
        if done:
            c = done[0]
            stage, name = due[c][0], ways[c][due[c][0]][0]
            line.append((name, c))
            now += COST[name]
            if stage + 1 < len(ways[c]):
                send(c, stage + 1)
            else:
                del due[c]
                ready.append(c)
        elif ready:
            c = min(ready)
            ready.remove(c)
            line.append(("work", c))
            now += WORK
            if c < sends:
                cross = max(now, cross) + CROSS
                landed[c] = cross + REACH
            else:
                kept.append(c)
        else:
            now = min(at for _, at in due.values())
        size = chunks - sends
        for c in list(kept):
            need = [landed.get(v, 1e9) for v in range(c - sends, sends, size)]
            if not ready and max(need, default=0.0) <= now:
                kept.remove(c)
                line.append(("close", c))
                now += LAST
    total = max([now] + list(landed.values()))
    return line + [("close", c) for c in kept], total


def table(count, scale):
    bins = FIRST_BIN + np.arange(count)
    shifts = np.arange(LAGS) - LAGS // 2
    angle = np.mod(shifts[:, None] * bins[None, :], WINDOW_LEN) * (2.0 * np.pi / WINDOW_LEN)
    return np.concatenate([np.cos(angle), -np.sin(angle)], axis=1) * scale


def factors(count, scale):
    full = table(count, 1.0)
    basis, sizes, _ = np.linalg.svd(full, full_matrices=False)
    rank = 8
    while rank < LAGS and np.sum(sizes[rank:] ** 2) > 1e-20 * np.sum(sizes ** 2):
        rank += 8
    basis = basis[:, :rank]
    return basis, (basis.T @ full).reshape(rank, 2, count) * scale


def group_of(n_chan):
    return max(min(8, n_chan // 2), 1)


def kernel(sizes, owner_hbm, row_hbm, spec_hbm, table_hbm, out_hbm, out_ref,
           owner_ref, row_ref, table_ref, spec_ref, pick, right, held, got1, got2, got_far, whole, cross, send, recv,
           lsem, csend, crecv, gsend, grecv, fsend, frecv, asend, arecv, xsend, xrecv):
    steps, per_step, bins, wins, chans, n_chan, n_tm, n_freq, size, rank_of = sizes
    peers = n_tm * n_freq
    per = per_step // peers
    block = steps * per
    total = steps * per_step
    chunks = total // size
    sends = (peers - 1) * block // size
    some = 64 // wins
    pairs = bins // (2 * some)
    group = group_of(n_chan)
    each = pairs // (2 * group)
    part, me = lax.axis_index("parts"), lax.axis_index("chan")
    tm, fq = lax.axis_index("tm"), lax.axis_index("freq")
    rank = tm * n_freq + fq
    half = me % 2
    spot = (me // 2) % group
    quads = max(group // 2, 1)
    side, deep = spot % 2, spot // 2
    slot = side * quads + deep if group > 1 else 0
    far = []
    while 2 * group * 2 ** len(far) < n_chan:
        far.append(2 * group * 2 ** len(far))

    def along(mask):
        other, d = me, 1
        while d <= mask:
            if mask & d:
                other = other + d * (1 - 2 * ((me // d) % 2))
            d *= 2
        return other

    def chan(mask):
        return (part, along(mask), tm, fq)

    def peer(p):
        other = (rank + p) % peers
        return (part, me, other // n_freq, other % n_freq)

    barrier = pltpu.get_barrier_semaphore()
    near = [1] + [2 * k for k in range(1, group)] + far
    for d in near:
        pl.semaphore_signal(barrier, inc=1, device_id=chan(d), device_id_type=MESH)
    for p in range(1, peers):
        pl.semaphore_signal(barrier, inc=1, device_id=peer(p), device_id_type=MESH)

    rows = 64 * pairs
    loads = 4

    def load(n):
        at = pl.ds(n * (rows // loads), rows // loads)
        return [pltpu.make_async_copy(spec_hbm.at[k, h, at], spec_ref.at[k, h, at], lsem.at[2 * (2 * n + h) + k])
                for h in range(2) for k in range(2)]

    small = [pltpu.make_async_copy(src, dst, lsem.at[16 + n]) for n, (src, dst) in enumerate(
        [(owner_hbm, owner_ref), (row_hbm, row_ref), (table_hbm, table_ref)])]
    for one in small[:2]:
        one.start()
    for n in range(loads):
        for one in load(n):
            one.start()
    small[2].start()
    for one in small:
        one.wait()

    channel = lax.broadcasted_iota(jnp.int32, (1, chans), 1)
    for p in range(1, peers + 1):
        for t in range(steps):
            held_here = owner_ref[t] == me
            for j in range(per):
                row = jnp.where(held_here, row_ref[t, ((rank + p) % peers) * per + j], -1)
                at = (p - 1) * block + t * per + j
                pick[pl.ds(at, 1), :] = (channel == row).astype(jnp.float32)
    chosen = pick[...].astype(jnp.bfloat16)

    def prepare(i):
        both = []
        for h in range(2):
            at = pl.ds(pl.multiple_of(i * 64, 64), 64)
            re = spec_ref[0, h, at, :].astype(jnp.float32)
            im = spec_ref[1, h, at, :].astype(jnp.float32)
            inverse = 1.0 / (jnp.sqrt(re * re + im * im) + WATER)
            re = (re * inverse).astype(jnp.bfloat16)
            im = (im * inverse).astype(jnp.bfloat16)
            right[i, h, :64, :chans] = re
            right[i, h, :64, chans:] = im
            right[i, h, 64:, :chans] = im
            right[i, h, 64:, chans:] = -re
            both += [re, im]
        got = lax.dot_general(chosen, jnp.concatenate(both, axis=0), (((1,), (1,)), ((), ())),
                              preferred_element_type=jnp.float32)
        for c in range(chunks):
            mine = got[c * size:(c + 1) * size]
            mine = jnp.concatenate([mine[:, :128], mine[:, 128:]], axis=0).astype(jnp.bfloat16)
            held[c, i // (pairs // 2), (i // each) % group, i % each] = mine

    def repeat(first, count, unroll, body):
        unroll = min(unroll, count)

        def some(i, carry):
            for r in range(unroll):
                body(first + i * unroll + r)
            return carry

        lax.fori_loop(0, count // unroll, some, 0)

    for n in range(loads):
        for one in load(n):
            one.wait()
        repeat(n * (pairs // loads), pairs // loads, 4, prepare)

    pl.semaphore_wait(barrier, len(near) + peers - 1)

    def core(c, back):
        if back:
            src = dst = whole.at[c, half]
        else:
            src, dst = held.at[c, 1 - half], got1.at[c]
        return pltpu.make_async_remote_copy(
            src_ref=src, dst_ref=dst, send_sem=csend.at[c, back], recv_sem=crecv.at[c, back],
            device_id=chan(1), device_id_type=MESH)

    def send_to(mask, c, n, src, dst, pair):
        to = chan(mask) if isinstance(mask, int) else (part, mask, tm, fq)
        return pltpu.make_async_remote_copy(
            src_ref=src, dst_ref=dst, send_sem=pair[0].at[c, n], recv_sem=pair[1].at[c, n],
            device_id=to, device_id_type=MESH)

    def around(k):
        other = (spot + k) % group
        return me + 2 * (other - spot), (other % 2) * quads + other // 2

    def scatter(c, k):
        to, at = around(k)
        return send_to(to, c, k - 1, held.at[c, half, at], got2.at[c, k - 1], (gsend, grecv))

    def gather(c, k):
        return send_to(around(k)[0], c, k - 1, whole.at[c, half, slot], whole.at[c, half, slot], (asend, arecv))

    mine_at = pl.ds(side * quads, quads)

    def scatter_side(c):
        return send_to(2, c, 0, held.at[c, half, pl.ds((1 - side) * quads, quads)], got2.at[c, pl.ds(0, quads)],
                       (gsend, grecv))

    def gather_side(c):
        return send_to(2, c, 0, whole.at[c, half, mine_at], whole.at[c, half, mine_at], (asend, arecv))

    def swap(c, n):
        return send_to(4 << n, c, n + 1, held.at[c, half, mine_at], got2.at[c, pl.ds((n + 1) * quads, quads)],
                       (gsend, grecv))

    def double(c, n, at, to):
        return send_to(far[n], c, n, held.at[c, half, at], got_far.at[c, n, to], (fsend, frecv))

    def start(copies):
        if COMM:
            for one in copies:
                one.start()

    def wait(copies):
        if COMM:
            for one in copies:
                one.wait()

    def several(make, c, count):
        return [make(c, k) for k in range(1, count)]

    def share(c, at, to, value):
        for n in range(len(far)):
            held[c, half, at] = value
            start([double(c, n, at, to)])
            wait([double(c, n, at, to)])
            value = value + got_far[c, n, to]
        whole[c, half, at] = value
        start(several(gather, c, group) if c in wide else [gather_side(c)])

    def core_in(c):
        wait([core(c, 0)])
        held[c, half] = held[c, half] + got1[c]
        start(several(scatter, c, group) if c in wide else [scatter_side(c)])

    def scatter_in(c):
        value = held[c, half, slot]
        for k in range(1, group):
            wait([scatter(c, k)])
            value = value + got2[c, k - 1]
        share(c, slot, 0, value)

    def quarter_in(c, n):
        value = held[c, half, mine_at] + got2[c, n * quads:(n + 1) * quads]
        if n < halvings:
            held[c, half, mine_at] = value
            start([swap(c, n)])
        else:
            share(c, mine_at, pl.ds(0, quads), value)

    def side_in(c):
        wait([scatter_side(c)])
        quarter_in(c, 0)

    def swap_in(n, c):
        wait([swap(c, n)])
        quarter_in(c, n + 1)

    def gather_in(c):
        wait(several(gather, c, group) if c in wide else [gather_side(c)])
        start([core(c, 1)])

    def back_in(c):
        wait([core(c, 1)])

    halvings = quads.bit_length() - 1
    kinds = [KINDS[c % len(KINDS)] if group > 1 else "W" for c in range(chunks)]
    wide = [c for c in range(chunks) if kinds[c] == "W"]

    lane = lax.broadcasted_iota(jnp.int32, (1, some, 128), 2)
    bin_of = lax.broadcasted_iota(jnp.int32, (1, some, 128), 1)
    mine = ((lane % 64) // wins) == bin_of

    def exchange(v):
        return pltpu.make_async_remote_copy(
            src_ref=send.at[v], dst_ref=recv.at[v], send_sem=xsend.at[v], recv_sem=xrecv.at[v],
            device_id=peer(v * size // block + 1), device_id_type=MESH)

    def multiply(u):
        def one(g):
            x = whole[u, g // (pairs // 2), (g // each) % group, g % each].astype(jnp.float32)
            got = []
            for h in range(2):
                wide = jnp.where(mine, x[h * size:(h + 1) * size, None, :], 0.0)
                left = wide.reshape(size * some, 128).astype(jnp.bfloat16)
                got.append(jnp.dot(left, right[g, h], preferred_element_type=jnp.float32).reshape(size, some, 2 * chans))
            for o in range(2):
                to = pl.ds(o * bins + g * 2 * some, 2 * some)
                value = jnp.concatenate([got[h][:, :, o * chans:(o + 1) * chans] for h in range(2)], axis=1)
                cross[:, to, :] = value.astype(jnp.bfloat16)

        if MUL:
            repeat(0, pairs, UNROLL, one)

    def lag(v, i):
        both = jnp.concatenate([cross[2 * i], cross[2 * i + 1]], axis=1)
        got = jnp.dot(table_ref[...], both, preferred_element_type=jnp.float32)
        if v < sends:
            both = jnp.concatenate([got[:, :chans], got[:, chans:]], axis=0)
            send[v, 2 * i * rank_of:2 * (i + 1) * rank_of] = both.astype(jnp.bfloat16)
        else:
            for r in range(2):
                out_ref[(v - sends) * size + 2 * i + r] = got[:, r * chans:(r + 1) * chans]

    def work(v):
        multiply(v)
        if LAG:
            for i in range(size // 2):
                lag(v, i)
        if v < sends and XCH:
            exchange(v).start()

    def put(w):
        at = pl.ds(w * size, size)
        return pltpu.make_async_copy(out_ref.at[at], out_hbm.at[at], lsem.at[19 + w])

    def close(v):
        w = v - sends
        for p in range(1, peers):
            v = (p - 1) * (block // size) + w
            if XCH:
                exchange(v).wait()
            for j in range(0, size, 2):
                value = recv[v, j * rank_of:(j + 2) * rank_of].astype(jnp.float32)
                for r in range(2):
                    at = w * size + j + r
                    out_ref[at] = out_ref[at] + value[r * rank_of:(r + 1) * rank_of]
        put(w).start()

    for c in range(chunks):
        start([core(c, 0)])
    acts = dict(core=core_in, scatter=scatter_in, side=side_in, near=functools.partial(swap_in, 0),
                next=functools.partial(swap_in, 1), gather=gather_in, back=back_in, work=work, close=close)
    for name, c in schedule(chunks, sends, kinds, halvings)[0]:
        acts[name](c)
    for w in range(block // size):
        put(w).wait()


def expand(coef_ref, basis_ref, out_ref):
    for j in range(coef_ref.shape[0]):
        value = coef_ref[j]
        high = value.astype(jnp.bfloat16)
        low = (value - high.astype(jnp.float32)).astype(jnp.bfloat16)
        both = jnp.concatenate([high, high, low], axis=0)
        out_ref[j] = lax.dot_general(both, basis_ref[...], (((0,), (0,)), ((), ())),
                                     preferred_element_type=jnp.float32)


def per_device(spectra, owners, source_rows):
    _, bins, wins, chans = spectra.shape
    steps, per_step = source_rows.shape
    n_chan, n_tm, n_freq = (lax.axis_size(a) for a in AXES[1:])
    peers = n_tm * n_freq
    per = per_step // peers
    block = steps * per
    size = min(8, block)
    chunks = steps * per_step // size
    some = 64 // wins
    pairs = bins // (2 * some)
    basis, rest = factors(bins * n_freq, 1.0 / (wins * n_tm))
    rank = basis.shape[1]
    rest = rest.reshape(rank, 2, n_freq, 2, pairs, some).transpose(2, 0, 1, 4, 3, 5).reshape(n_freq, rank, 2 * bins)
    rest = jnp.asarray(rest.astype(jnp.bfloat16))
    rest = lax.dynamic_index_in_dim(rest, lax.axis_index("freq"), 0, False) if n_freq > 1 else rest[0]
    high = basis.T.astype(np.float32).astype(jnp.bfloat16)
    low = (basis.T - high.astype(np.float64)).astype(jnp.bfloat16)
    spread = jnp.asarray(np.concatenate([high, low, high], axis=0))
    group = group_of(n_chan)
    far = max((n_chan // (2 * group)).bit_length() - 1, 1)
    sizes = (steps, per_step, bins, wins, chans, n_chan, n_tm, n_freq, size, rank)
    bf16, f32 = jnp.bfloat16, jnp.float32
    piece = (pairs // (2 * group), 2 * size, 128)
    sends = max((peers - 1) * block // size, 1)
    links = max(group - 1, 3)
    quads = max(group // 2, 1)
    dma = pltpu.SemaphoreType.DMA
    coef = pl.pallas_call(
        functools.partial(kernel, sizes),
        out_shape=jax.ShapeDtypeStruct((block, rank, chans), f32),
        in_specs=[pl.BlockSpec(memory_space=pl.ANY)] * 4,
        out_specs=pl.BlockSpec(memory_space=pl.ANY),
        scratch_shapes=[
            pltpu.VMEM((block, rank, chans), f32),
            pltpu.SMEM((steps,), jnp.int32),
            pltpu.SMEM((steps, per_step), jnp.int32),
            pltpu.VMEM((rank, 2 * bins), bf16),
            pltpu.VMEM((2, 2, bins * wins // 2, chans), bf16),
            pltpu.VMEM((steps * per_step, chans), f32),
            pltpu.VMEM((pairs, 2, 128, 2 * chans), bf16),
            pltpu.VMEM((chunks, 2, group) + piece, bf16),
            pltpu.VMEM((chunks, group) + piece, bf16),
            pltpu.VMEM((chunks, max(3 * quads, links)) + piece, bf16),
            pltpu.VMEM((chunks, far, quads) + piece, bf16),
            pltpu.VMEM((chunks, 2, group) + piece, bf16),
            pltpu.VMEM((size, 2 * bins, chans), bf16),
            pltpu.VMEM((sends, size * rank, chans), bf16),
            pltpu.VMEM((sends, size * rank, chans), bf16),
            dma((19 + block // size,)), dma((chunks, 2)), dma((chunks, 2)), dma((chunks, links)), dma((chunks, links)),
            dma((chunks, far)), dma((chunks, far)), dma((chunks, links)), dma((chunks, links)),
            dma((sends,)), dma((sends,)),
        ],
        compiler_params=pltpu.CompilerParams(collective_id=0, has_side_effects=True),
    )(owners, source_rows, spectra.reshape(2, 2, bins * wins // 2, chans), rest)
    tile = max(block // 2, 1)
    out = pl.pallas_call(
        expand,
        out_shape=jax.ShapeDtypeStruct((block, chans, LAGS), f32),
        grid=(block // tile,),
        in_specs=[pl.BlockSpec((tile, rank, chans), lambda i: (i, 0, 0)),
                  pl.BlockSpec((3 * rank, LAGS), lambda i: (0, 0))],
        out_specs=pl.BlockSpec((tile, chans, LAGS), lambda i: (i, 0, 0)),
    )(coef, spread)
    return out.reshape(steps, per, chans, LAGS)


def solution(mesh):
    placed = (P(None, "freq", "tm", ("parts", "chan")), P("parts"), P("parts", None))
    return jax.shard_map(
        per_device,
        mesh=mesh,
        in_specs=placed,
        out_specs=P(None, ("tm", "freq"), ("parts", "chan"), None),
        check_vma=False,
    )
```

```python
import functools

import jax
import jax.numpy as jnp
import numpy as np
from jax import lax
from jax.experimental import pallas as pl
from jax.experimental.pallas import tpu as pltpu
from jax.sharding import PartitionSpec as P

WINDOW_LEN = 4096
FIRST_BIN = 64
LAGS = 128
WATER = 0.5
AXES = ("parts", "chan", "tm", "freq")
MESH = pl.DeviceIdType.MESH
KINDS = "NWWWNNNN"
UNROLL = 32
WAYS = {
    "W": (("core", 1.0, (0.1, 0, 0, 0)), ("scatter", 2.9, (0, 0.6, 0.585, 0.975)), ("gather", 2.9, (0, 0.6, 0.585, 0.975)),
          ("back", 1.0, (0.1, 0, 0, 0))),
    "N": (("core", 1.0, (0.1, 0, 0, 0)), ("side", 2.1, (0, 0.6, 0, 0)), ("near", 2.1, (0, 0, 0.39, 0)),
          ("next", 2.5, (0, 0, 0.39, 0.78)), ("gather", 2.1, (0, 0.6, 0, 0)), ("back", 1.0, (0.1, 0, 0, 0))),
}
COST = {"core": 0.2, "scatter": 0.35, "side": 0.15, "near": 0.15, "next": 0.15, "gather": 0.1, "back": 0.05}
WORK, LAST, CROSS, REACH = 1.05, 0.15, 2.15, 2.2


def schedule(chunks, sends, kinds, halvings):
    ways = []
    for c in range(chunks):
        way = WAYS[kinds[c]]
        ways.append([one for one in way if one[0] not in ("near", "next")[halvings:]])
    free, cross, now = [0.0] * 4, 0.0, 0.0
    due, line, ready, kept, landed = {}, [], [], [], {}

    def send(c, stage):
        _, wait, loads = ways[c][stage]
        end = now
        for n, load in enumerate(loads):
            if load:
                free[n] = max(now, free[n]) + load
                end = max(end, free[n])
        due[c] = (stage, end + wait)

    for c in range(chunks):
        send(c, 0)
    while due or ready:
        done = [c for c in sorted(due) if due[c][1] <= now]
        if done:
            c = done[0]
            stage, name = due[c][0], ways[c][due[c][0]][0]
            line.append((name, c))
            now += COST[name]
            if stage + 1 < len(ways[c]):
                send(c, stage + 1)
            else:
                del due[c]
                ready.append(c)
        elif ready:
            c = min(ready)
            ready.remove(c)
            line.append(("work", c))
            now += WORK
            if c < sends:
                cross = max(now, cross) + CROSS
                landed[c] = cross + REACH
            else:
                kept.append(c)
        else:
            now = min(at for _, at in due.values())
        size = chunks - sends
        for c in list(kept):
            need = [landed.get(v, 1e9) for v in range(c - sends, sends, size)]
            if not ready and max(need, default=0.0) <= now:
                kept.remove(c)
                line.append(("close", c))
                now += LAST
    total = max([now] + list(landed.values()))
    return line + [("close", c) for c in kept], total


def table(count, scale):
    bins = FIRST_BIN + np.arange(count)
    shifts = np.arange(LAGS) - LAGS // 2
    angle = np.mod(shifts[:, None] * bins[None, :], WINDOW_LEN) * (2.0 * np.pi / WINDOW_LEN)
    return np.concatenate([np.cos(angle), -np.sin(angle)], axis=1) * scale


def factors(count, scale):
    full = table(count, 1.0)
    basis, sizes, _ = np.linalg.svd(full, full_matrices=False)
    rank = 8
    while rank < LAGS and np.sum(sizes[rank:] ** 2) > 1e-20 * np.sum(sizes ** 2):
        rank += 8
    basis = basis[:, :rank]
    return basis, (basis.T @ full).reshape(rank, 2, count) * scale


def group_of(n_chan):
    return max(min(8, n_chan // 2), 1)


def kernel(sizes, owner_hbm, row_hbm, spec_hbm, table_hbm, out_hbm, out_ref,
           owner_ref, row_ref, table_ref, spec_ref, pick, right, held, got1, got2, got_far, whole, cross, send, recv,
           lsem, csend, crecv, gsend, grecv, fsend, frecv, asend, arecv, xsend, xrecv):
    steps, per_step, bins, wins, chans, n_chan, n_tm, n_freq, size, rank_of = sizes
    peers = n_tm * n_freq
    per = per_step // peers
    block = steps * per
    total = steps * per_step
    chunks = total // size
    sends = (peers - 1) * block // size
    some = 64 // wins
    pairs = bins // (2 * some)
    group = group_of(n_chan)
    each = pairs // (2 * group)
    part, me = lax.axis_index("parts"), lax.axis_index("chan")
    tm, fq = lax.axis_index("tm"), lax.axis_index("freq")
    rank = tm * n_freq + fq
    half = me % 2
    spot = (me // 2) % group
    quads = max(group // 2, 1)
    side, deep = spot % 2, spot // 2
    slot = side * quads + deep if group > 1 else 0
    far = []
    while 2 * group * 2 ** len(far) < n_chan:
        far.append(2 * group * 2 ** len(far))

    def along(mask):
        other, d = me, 1
        while d <= mask:
            if mask & d:
                other = other + d * (1 - 2 * ((me // d) % 2))
            d *= 2
        return other

    def chan(mask):
        return (part, along(mask), tm, fq)

    def peer(p):
        other = (rank + p) % peers
        return (part, me, other // n_freq, other % n_freq)

    barrier = pltpu.get_barrier_semaphore()
    near = [1] + [2 * k for k in range(1, group)] + far
    for d in near:
        pl.semaphore_signal(barrier, inc=1, device_id=chan(d), device_id_type=MESH)
    for p in range(1, peers):
        pl.semaphore_signal(barrier, inc=1, device_id=peer(p), device_id_type=MESH)

    rows = 64 * pairs
    loads = 4

    def load(n):
        at = pl.ds(n * (rows // loads), rows // loads)
        return [pltpu.make_async_copy(spec_hbm.at[k, h, at], spec_ref.at[k, h, at], lsem.at[2 * (2 * n + h) + k])
                for h in range(2) for k in range(2)]

    small = [pltpu.make_async_copy(src, dst, lsem.at[16 + n]) for n, (src, dst) in enumerate(
        [(owner_hbm, owner_ref), (row_hbm, row_ref), (table_hbm, table_ref)])]
    for one in small[:2]:
        one.start()
    for n in range(loads):
        for one in load(n):
            one.start()
    small[2].start()
    for one in small:
        one.wait()

    channel = lax.broadcasted_iota(jnp.int32, (1, chans), 1)
    for p in range(1, peers + 1):
        for t in range(steps):
            held_here = owner_ref[t] == me
            for j in range(per):
                row = jnp.where(held_here, row_ref[t, ((rank + p) % peers) * per + j], -1)
                at = (p - 1) * block + t * per + j
                pick[pl.ds(at, 1), :] = (channel == row).astype(jnp.float32)
    chosen = pick[...].astype(jnp.bfloat16)

    def prepare(i):
        both = []
        for h in range(2):
            at = pl.ds(pl.multiple_of(i * 64, 64), 64)
            re = spec_ref[0, h, at, :].astype(jnp.float32)
            im = spec_ref[1, h, at, :].astype(jnp.float32)
            inverse = 1.0 / (jnp.sqrt(re * re + im * im) + WATER)
            re = (re * inverse).astype(jnp.bfloat16)
            im = (im * inverse).astype(jnp.bfloat16)
            right[i, h, :64, :chans] = re
            right[i, h, :64, chans:] = im
            right[i, h, 64:, :chans] = im
            right[i, h, 64:, chans:] = -re
            both += [re, im]
        got = lax.dot_general(chosen, jnp.concatenate(both, axis=0), (((1,), (1,)), ((), ())),
                              preferred_element_type=jnp.float32)
        for c in range(chunks):
            mine = got[c * size:(c + 1) * size]
            mine = jnp.concatenate([mine[:, :128], mine[:, 128:]], axis=0).astype(jnp.bfloat16)
            held[c, i // (pairs // 2), (i // each) % group, i % each] = mine

    def repeat(first, count, unroll, body):
        unroll = min(unroll, count)

        def some(i, carry):
            for r in range(unroll):
                body(first + i * unroll + r)
            return carry

        lax.fori_loop(0, count // unroll, some, 0)

    for n in range(loads):
        for one in load(n):
            one.wait()
        repeat(n * (pairs // loads), pairs // loads, 4, prepare)

    pl.semaphore_wait(barrier, len(near) + peers - 1)

    def core(c, back):
        if back:
            src = dst = whole.at[c, half]
        else:
            src, dst = held.at[c, 1 - half], got1.at[c]
        return pltpu.make_async_remote_copy(
            src_ref=src, dst_ref=dst, send_sem=csend.at[c, back], recv_sem=crecv.at[c, back],
            device_id=chan(1), device_id_type=MESH)

    def send_to(mask, c, n, src, dst, pair):
        to = chan(mask) if isinstance(mask, int) else (part, mask, tm, fq)
        return pltpu.make_async_remote_copy(
            src_ref=src, dst_ref=dst, send_sem=pair[0].at[c, n], recv_sem=pair[1].at[c, n],
            device_id=to, device_id_type=MESH)

    def around(k):
        other = (spot + k) % group
        return me + 2 * (other - spot), (other % 2) * quads + other // 2

    def scatter(c, k):
        to, at = around(k)
        return send_to(to, c, k - 1, held.at[c, half, at], got2.at[c, k - 1], (gsend, grecv))

    def gather(c, k):
        return send_to(around(k)[0], c, k - 1, whole.at[c, half, slot], whole.at[c, half, slot], (asend, arecv))

    mine_at = pl.ds(side * quads, quads)

    def scatter_side(c):
        return send_to(2, c, 0, held.at[c, half, pl.ds((1 - side) * quads, quads)], got2.at[c, pl.ds(0, quads)],
                       (gsend, grecv))

    def gather_side(c):
        return send_to(2, c, 0, whole.at[c, half, mine_at], whole.at[c, half, mine_at], (asend, arecv))

    def swap(c, n):
        return send_to(4 << n, c, n + 1, held.at[c, half, mine_at], got2.at[c, pl.ds((n + 1) * quads, quads)],
                       (gsend, grecv))

    def double(c, n, at, to):
        return send_to(far[n], c, n, held.at[c, half, at], got_far.at[c, n, to], (fsend, frecv))

    def start(copies):
        for one in copies:
            one.start()

    def wait(copies):
        for one in copies:
            one.wait()

    def several(make, c, count):
        return [make(c, k) for k in range(1, count)]

    def share(c, at, to, value):
        for n in range(len(far)):
            held[c, half, at] = value
            start([double(c, n, at, to)])
            wait([double(c, n, at, to)])
            value = value + got_far[c, n, to]
        whole[c, half, at] = value
        start(several(gather, c, group) if c in wide else [gather_side(c)])

    def core_in(c):
        wait([core(c, 0)])
        held[c, half] = held[c, half] + got1[c]
        start(several(scatter, c, group) if c in wide else [scatter_side(c)])

    def scatter_in(c):
        value = held[c, half, slot]
        for k in range(1, group):
            wait([scatter(c, k)])
            value = value + got2[c, k - 1]
        share(c, slot, 0, value)

    def quarter_in(c, n):
        value = held[c, half, mine_at] + got2[c, n * quads:(n + 1) * quads]
        if n < halvings:
            held[c, half, mine_at] = value
            start([swap(c, n)])
        else:
            share(c, mine_at, pl.ds(0, quads), value)

    def side_in(c):
        wait([scatter_side(c)])
        quarter_in(c, 0)

    def swap_in(n, c):
        wait([swap(c, n)])
        quarter_in(c, n + 1)

    def gather_in(c):
        wait(several(gather, c, group) if c in wide else [gather_side(c)])
        start([core(c, 1)])

    def back_in(c):
        wait([core(c, 1)])

    halvings = quads.bit_length() - 1
    kinds = [KINDS[c % len(KINDS)] if group > 1 else "W" for c in range(chunks)]
    wide = [c for c in range(chunks) if kinds[c] == "W"]

    lane = lax.broadcasted_iota(jnp.int32, (1, some, 128), 2)
    bin_of = lax.broadcasted_iota(jnp.int32, (1, some, 128), 1)
    mine = ((lane % 64) // wins) == bin_of

    def exchange(v):
        return pltpu.make_async_remote_copy(
            src_ref=send.at[v], dst_ref=recv.at[v], send_sem=xsend.at[v], recv_sem=xrecv.at[v],
            device_id=peer(v * size // block + 1), device_id_type=MESH)

    def multiply(u):
        def one(g):
            x = whole[u, g // (pairs // 2), (g // each) % group, g % each].astype(jnp.float32)
            got = []
            for h in range(2):
                wide = jnp.where(mine, x[h * size:(h + 1) * size, None, :], 0.0)
                left = wide.reshape(size * some, 128).astype(jnp.bfloat16)
                got.append(jnp.dot(left, right[g, h], preferred_element_type=jnp.float32).reshape(size, some, 2 * chans))
            for o in range(2):
                to = pl.ds(o * bins + g * 2 * some, 2 * some)
                value = jnp.concatenate([got[h][:, :, o * chans:(o + 1) * chans] for h in range(2)], axis=1)
                cross[:, to, :] = value.astype(jnp.bfloat16)

        repeat(0, pairs, UNROLL, one)

    def lag(v, i):
        both = jnp.concatenate([cross[2 * i], cross[2 * i + 1]], axis=1)
        got = jnp.dot(table_ref[...], both, preferred_element_type=jnp.float32)
        if v < sends:
            both = jnp.concatenate([got[:, :chans], got[:, chans:]], axis=0)
            send[v, 2 * i * rank_of:2 * (i + 1) * rank_of] = both.astype(jnp.bfloat16)
        else:
            for r in range(2):
                out_ref[(v - sends) * size + 2 * i + r] = got[:, r * chans:(r + 1) * chans]

    def work(v):
        multiply(v)
        for i in range(size // 2):
            lag(v, i)
        if v < sends:
            exchange(v).start()

    def put(w):
        at = pl.ds(w * size, size)
        return pltpu.make_async_copy(out_ref.at[at], out_hbm.at[at], lsem.at[19 + w])

    def close(v):
        w = v - sends
        for p in range(1, peers):
            v = (p - 1) * (block // size) + w
            exchange(v).wait()
            for j in range(0, size, 2):
                value = recv[v, j * rank_of:(j + 2) * rank_of].astype(jnp.float32)
                for r in range(2):
                    at = w * size + j + r
                    out_ref[at] = out_ref[at] + value[r * rank_of:(r + 1) * rank_of]
        put(w).start()

    for c in range(chunks):
        start([core(c, 0)])
    acts = dict(core=core_in, scatter=scatter_in, side=side_in, near=functools.partial(swap_in, 0),
                next=functools.partial(swap_in, 1), gather=gather_in, back=back_in, work=work, close=close)
    for name, c in schedule(chunks, sends, kinds, halvings)[0]:
        acts[name](c)
    for w in range(block // size):
        put(w).wait()


def expand(coef_ref, basis_ref, out_ref):
    for j in range(coef_ref.shape[0]):
        value = coef_ref[j]
        high = value.astype(jnp.bfloat16)
        low = (value - high.astype(jnp.float32)).astype(jnp.bfloat16)
        both = jnp.concatenate([high, high, low], axis=0)
        out_ref[j] = lax.dot_general(both, basis_ref[...], (((0,), (0,)), ((), ())),
                                     preferred_element_type=jnp.float32)


def per_device(spectra, owners, source_rows):
    _, bins, wins, chans = spectra.shape
    steps, per_step = source_rows.shape
    n_chan, n_tm, n_freq = (lax.axis_size(a) for a in AXES[1:])
    peers = n_tm * n_freq
    per = per_step // peers
    block = steps * per
    size = min(8, block)
    chunks = steps * per_step // size
    some = 64 // wins
    pairs = bins // (2 * some)
    basis, rest = factors(bins * n_freq, 1.0 / (wins * n_tm))
    rank = basis.shape[1]
    rest = rest.reshape(rank, 2, n_freq, 2, pairs, some).transpose(2, 0, 1, 4, 3, 5).reshape(n_freq, rank, 2 * bins)
    rest = jnp.asarray(rest.astype(jnp.bfloat16))
    rest = lax.dynamic_index_in_dim(rest, lax.axis_index("freq"), 0, False) if n_freq > 1 else rest[0]
    high = basis.T.astype(np.float32).astype(jnp.bfloat16)
    low = (basis.T - high.astype(np.float64)).astype(jnp.bfloat16)
    spread = jnp.asarray(np.concatenate([high, low, high], axis=0))
    group = group_of(n_chan)
    far = max((n_chan // (2 * group)).bit_length() - 1, 1)
    sizes = (steps, per_step, bins, wins, chans, n_chan, n_tm, n_freq, size, rank)
    bf16, f32 = jnp.bfloat16, jnp.float32
    piece = (pairs // (2 * group), 2 * size, 128)
    sends = max((peers - 1) * block // size, 1)
    links = max(group - 1, 3)
    quads = max(group // 2, 1)
    dma = pltpu.SemaphoreType.DMA
    coef = pl.pallas_call(
        functools.partial(kernel, sizes),
        out_shape=jax.ShapeDtypeStruct((block, rank, chans), f32),
        in_specs=[pl.BlockSpec(memory_space=pl.ANY)] * 4,
        out_specs=pl.BlockSpec(memory_space=pl.ANY),
        scratch_shapes=[
            pltpu.VMEM((block, rank, chans), f32),
            pltpu.SMEM((steps,), jnp.int32),
            pltpu.SMEM((steps, per_step), jnp.int32),
            pltpu.VMEM((rank, 2 * bins), bf16),
            pltpu.VMEM((2, 2, bins * wins // 2, chans), bf16),
            pltpu.VMEM((steps * per_step, chans), f32),
            pltpu.VMEM((pairs, 2, 128, 2 * chans), bf16),
            pltpu.VMEM((chunks, 2, group) + piece, bf16),
            pltpu.VMEM((chunks, group) + piece, bf16),
            pltpu.VMEM((chunks, max(3 * quads, links)) + piece, bf16),
            pltpu.VMEM((chunks, far, quads) + piece, bf16),
            pltpu.VMEM((chunks, 2, group) + piece, bf16),
            pltpu.VMEM((size, 2 * bins, chans), bf16),
            pltpu.VMEM((sends, size * rank, chans), bf16),
            pltpu.VMEM((sends, size * rank, chans), bf16),
            dma((19 + block // size,)), dma((chunks, 2)), dma((chunks, 2)), dma((chunks, links)), dma((chunks, links)),
            dma((chunks, far)), dma((chunks, far)), dma((chunks, links)), dma((chunks, links)),
            dma((sends,)), dma((sends,)),
        ],
        compiler_params=pltpu.CompilerParams(collective_id=0, has_side_effects=True),
    )(owners, source_rows, spectra.reshape(2, 2, bins * wins // 2, chans), rest)
    tile = max(block // 2, 1)
    out = pl.pallas_call(
        expand,
        out_shape=jax.ShapeDtypeStruct((block, chans, LAGS), f32),
        grid=(block // tile,),
        in_specs=[pl.BlockSpec((tile, rank, chans), lambda i: (i, 0, 0)),
                  pl.BlockSpec((3 * rank, LAGS), lambda i: (0, 0))],
        out_specs=pl.BlockSpec((tile, chans, LAGS), lambda i: (i, 0, 0)),
    )(coef, spread)
    return out.reshape(steps, per, chans, LAGS)


def solution(mesh):
    placed = (P(None, "freq", "tm", ("parts", "chan")), P("parts"), P("parts", None))
    return jax.shard_map(
        per_device,
        mesh=mesh,
        in_specs=placed,
        out_specs=P(None, ("tm", "freq"), ("parts", "chan"), None),
        check_vma=False,
    )
```

```python
import functools

import jax
import jax.numpy as jnp
import numpy as np
from jax import lax
from jax.experimental import pallas as pl
from jax.experimental.pallas import tpu as pltpu
from jax.sharding import PartitionSpec as P

WINDOW_LEN = 4096
FIRST_BIN = 64
LAGS = 128
WATER = 0.5
AXES = ("parts", "chan", "tm", "freq")
MESH = pl.DeviceIdType.MESH
KINDS = "NWWWNNNN"
UNROLL = 32
WAYS = {
    "W": (("core", 1.0, (0.1, 0, 0, 0)), ("scatter", 2.9, (0, 0.45, 0.585, 0.975)), ("gather", 2.9, (0, 0.45, 0.585, 0.975)),
          ("back", 1.0, (0.1, 0, 0, 0))),
    "N": (("core", 1.0, (0.1, 0, 0, 0)), ("side", 2.1, (0, 0.45, 0, 0)), ("near", 2.1, (0, 0, 0.39, 0)),
          ("next", 2.5, (0, 0, 0.39, 0.78)), ("gather", 2.1, (0, 0.45, 0, 0)), ("back", 1.0, (0.1, 0, 0, 0))),
}
COST = {"core": 0.2, "scatter": 0.35, "side": 0.15, "near": 0.15, "next": 0.15, "gather": 0.1, "back": 0.05}
WORK, LAST, CROSS, REACH = 1.05, 0.15, 2.15, 2.2


def schedule(chunks, sends, kinds, halvings):
    ways = []
    for c in range(chunks):
        way = WAYS[kinds[c]]
        ways.append([one for one in way if one[0] not in ("near", "next")[halvings:]])
    free, cross, now = [0.0] * 4, 0.0, 0.0
    due, line, ready, kept, landed = {}, [], [], [], {}

    def send(c, stage):
        _, wait, loads = ways[c][stage]
        end = now
        for n, load in enumerate(loads):
            if load:
                free[n] = max(now, free[n]) + load
                end = max(end, free[n])
        due[c] = (stage, end + wait)

    for c in range(chunks):
        send(c, 0)
    while due or ready:
        done = [c for c in sorted(due) if due[c][1] <= now]
        if done:
            c = done[0]
            stage, name = due[c][0], ways[c][due[c][0]][0]
            line.append((name, c))
            now += COST[name]
            if stage + 1 < len(ways[c]):
                send(c, stage + 1)
            else:
                del due[c]
                ready.append(c)
        elif ready:
            c = min(ready)
            ready.remove(c)
            line.append(("work", c))
            now += WORK
            if c < sends:
                cross = max(now, cross) + CROSS
                landed[c] = cross + REACH
            else:
                kept.append(c)
        else:
            now = min(at for _, at in due.values())
        size = chunks - sends
        for c in list(kept):
            need = [landed.get(v, 1e9) for v in range(c - sends, sends, size)]
            if not ready and max(need, default=0.0) <= now:
                kept.remove(c)
                line.append(("close", c))
                now += LAST
    total = max([now] + list(landed.values()))
    return line + [("close", c) for c in kept], total


def table(count, scale):
    bins = FIRST_BIN + np.arange(count)
    shifts = np.arange(LAGS) - LAGS // 2
    angle = np.mod(shifts[:, None] * bins[None, :], WINDOW_LEN) * (2.0 * np.pi / WINDOW_LEN)
    return np.concatenate([np.cos(angle), -np.sin(angle)], axis=1) * scale


def factors(count, scale):
    full = table(count, 1.0)
    basis, sizes, _ = np.linalg.svd(full, full_matrices=False)
    rank = 8
    while rank < LAGS and np.sum(sizes[rank:] ** 2) > 1e-20 * np.sum(sizes ** 2):
        rank += 8
    basis = basis[:, :rank]
    return basis, (basis.T @ full).reshape(rank, 2, count) * scale


def group_of(n_chan):
    return max(min(8, n_chan // 2), 1)


def kernel(sizes, owner_hbm, row_hbm, spec_hbm, table_hbm, out_hbm, out_ref,
           owner_ref, row_ref, table_ref, spec_ref, pick, right, held, got1, got2, got_far, whole, cross, send, recv,
           lsem, csend, crecv, gsend, grecv, fsend, frecv, asend, arecv, xsend, xrecv):
    steps, per_step, bins, wins, chans, n_chan, n_tm, n_freq, size, rank_of = sizes
    peers = n_tm * n_freq
    per = per_step // peers
    block = steps * per
    total = steps * per_step
    chunks = total // size
    sends = (peers - 1) * block // size
    some = 64 // wins
    pairs = bins // (2 * some)
    group = group_of(n_chan)
    each = pairs // (2 * group)
    part, me = lax.axis_index("parts"), lax.axis_index("chan")
    tm, fq = lax.axis_index("tm"), lax.axis_index("freq")
    rank = tm * n_freq + fq
    half = me % 2
    spot = (me // 2) % group
    quads = max(group // 2, 1)
    side, deep = spot % 2, spot // 2
    slot = side * quads + deep if group > 1 else 0
    far = []
    while 2 * group * 2 ** len(far) < n_chan:
        far.append(2 * group * 2 ** len(far))

    def along(mask):
        other, d = me, 1
        while d <= mask:
            if mask & d:
                other = other + d * (1 - 2 * ((me // d) % 2))
            d *= 2
        return other

    def chan(mask):
        return (part, along(mask), tm, fq)

    def peer(p):
        other = (rank + p) % peers
        return (part, me, other // n_freq, other % n_freq)

    barrier = pltpu.get_barrier_semaphore()
    near = [1] + [2 * k for k in range(1, group)] + far
    for d in near:
        pl.semaphore_signal(barrier, inc=1, device_id=chan(d), device_id_type=MESH)
    for p in range(1, peers):
        pl.semaphore_signal(barrier, inc=1, device_id=peer(p), device_id_type=MESH)

    rows = 64 * pairs
    loads = 4

    def load(n):
        at = pl.ds(n * (rows // loads), rows // loads)
        return [pltpu.make_async_copy(spec_hbm.at[k, h, at], spec_ref.at[k, h, at], lsem.at[2 * (2 * n + h) + k])
                for h in range(2) for k in range(2)]

    small = [pltpu.make_async_copy(src, dst, lsem.at[16 + n]) for n, (src, dst) in enumerate(
        [(owner_hbm, owner_ref), (row_hbm, row_ref), (table_hbm, table_ref)])]
    for one in small[:2]:
        one.start()
    for n in range(loads):
        for one in load(n):
            one.start()
    small[2].start()
    for one in small:
        one.wait()

    channel = lax.broadcasted_iota(jnp.int32, (1, chans), 1)
    for p in range(1, peers + 1):
        for t in range(steps):
            held_here = owner_ref[t] == me
            for j in range(per):
                row = jnp.where(held_here, row_ref[t, ((rank + p) % peers) * per + j], -1)
                at = (p - 1) * block + t * per + j
                pick[pl.ds(at, 1), :] = (channel == row).astype(jnp.float32)
    chosen = pick[...].astype(jnp.bfloat16)

    def prepare(i):
        both = []
        for h in range(2):
            at = pl.ds(pl.multiple_of(i * 64, 64), 64)
            re = spec_ref[0, h, at, :].astype(jnp.float32)
            im = spec_ref[1, h, at, :].astype(jnp.float32)
            inverse = 1.0 / (jnp.sqrt(re * re + im * im) + WATER)
            re = (re * inverse).astype(jnp.bfloat16)
            im = (im * inverse).astype(jnp.bfloat16)
            right[i, h, :64, :chans] = re
            right[i, h, :64, chans:] = im
            right[i, h, 64:, :chans] = im
            right[i, h, 64:, chans:] = -re
            both += [re, im]
        got = lax.dot_general(chosen, jnp.concatenate(both, axis=0), (((1,), (1,)), ((), ())),
                              preferred_element_type=jnp.float32)
        for c in range(chunks):
            mine = got[c * size:(c + 1) * size]
            mine = jnp.concatenate([mine[:, :128], mine[:, 128:]], axis=0).astype(jnp.bfloat16)
            held[c, i // (pairs // 2), (i // each) % group, i % each] = mine

    def repeat(first, count, unroll, body):
        unroll = min(unroll, count)

        def some(i, carry):
            for r in range(unroll):
                body(first + i * unroll + r)
            return carry

        lax.fori_loop(0, count // unroll, some, 0)

    for n in range(loads):
        for one in load(n):
            one.wait()
        repeat(n * (pairs // loads), pairs // loads, 4, prepare)

    pl.semaphore_wait(barrier, len(near) + peers - 1)

    def core(c, back):
        if back:
            src = dst = whole.at[c, half]
        else:
            src, dst = held.at[c, 1 - half], got1.at[c]
        return pltpu.make_async_remote_copy(
            src_ref=src, dst_ref=dst, send_sem=csend.at[c, back], recv_sem=crecv.at[c, back],
            device_id=chan(1), device_id_type=MESH)

    def send_to(mask, c, n, src, dst, pair):
        to = chan(mask) if isinstance(mask, int) else (part, mask, tm, fq)
        return pltpu.make_async_remote_copy(
            src_ref=src, dst_ref=dst, send_sem=pair[0].at[c, n], recv_sem=pair[1].at[c, n],
            device_id=to, device_id_type=MESH)

    def around(k):
        other = (spot + k) % group
        return me + 2 * (other - spot), (other % 2) * quads + other // 2

    def scatter(c, k):
        to, at = around(k)
        return send_to(to, c, k - 1, held.at[c, half, at], got2.at[c, k - 1], (gsend, grecv))

    def gather(c, k):
        return send_to(around(k)[0], c, k - 1, whole.at[c, half, slot], whole.at[c, half, slot], (asend, arecv))

    mine_at = pl.ds(side * quads, quads)

    def scatter_side(c):
        return send_to(2, c, 0, held.at[c, half, pl.ds((1 - side) * quads, quads)], got2.at[c, pl.ds(0, quads)],
                       (gsend, grecv))

    def gather_side(c):
        return send_to(2, c, 0, whole.at[c, half, mine_at], whole.at[c, half, mine_at], (asend, arecv))

    def swap(c, n):
        return send_to(4 << n, c, n + 1, held.at[c, half, mine_at], got2.at[c, pl.ds((n + 1) * quads, quads)],
                       (gsend, grecv))

    def double(c, n, at, to):
        return send_to(far[n], c, n, held.at[c, half, at], got_far.at[c, n, to], (fsend, frecv))

    def start(copies):
        for one in copies:
            one.start()

    def wait(copies):
        for one in copies:
            one.wait()

    def several(make, c, count):
        return [make(c, k) for k in range(1, count)]

    def share(c, at, to, value):
        for n in range(len(far)):
            held[c, half, at] = value
            start([double(c, n, at, to)])
            wait([double(c, n, at, to)])
            value = value + got_far[c, n, to]
        whole[c, half, at] = value
        start(several(gather, c, group) if c in wide else [gather_side(c)])

    def core_in(c):
        wait([core(c, 0)])
        held[c, half] = held[c, half] + got1[c]
        start(several(scatter, c, group) if c in wide else [scatter_side(c)])

    def scatter_in(c):
        value = held[c, half, slot]
        for k in range(1, group):
            wait([scatter(c, k)])
            value = value + got2[c, k - 1]
        share(c, slot, 0, value)

    def quarter_in(c, n):
        value = held[c, half, mine_at] + got2[c, n * quads:(n + 1) * quads]
        if n < halvings:
            held[c, half, mine_at] = value
            start([swap(c, n)])
        else:
            share(c, mine_at, pl.ds(0, quads), value)

    def side_in(c):
        wait([scatter_side(c)])
        quarter_in(c, 0)

    def swap_in(n, c):
        wait([swap(c, n)])
        quarter_in(c, n + 1)

    def gather_in(c):
        wait(several(gather, c, group) if c in wide else [gather_side(c)])
        start([core(c, 1)])

    def back_in(c):
        wait([core(c, 1)])

    halvings = quads.bit_length() - 1
    kinds = [KINDS[c % len(KINDS)] if group > 1 else "W" for c in range(chunks)]
    wide = [c for c in range(chunks) if kinds[c] == "W"]

    lane = lax.broadcasted_iota(jnp.int32, (1, some, 128), 2)
    bin_of = lax.broadcasted_iota(jnp.int32, (1, some, 128), 1)
    mine = ((lane % 64) // wins) == bin_of

    def exchange(v):
        return pltpu.make_async_remote_copy(
            src_ref=send.at[v], dst_ref=recv.at[v], send_sem=xsend.at[v], recv_sem=xrecv.at[v],
            device_id=peer(v * size // block + 1), device_id_type=MESH)

    def multiply(u):
        def one(g):
            x = whole[u, g // (pairs // 2), (g // each) % group, g % each].astype(jnp.float32)
            got = []
            for h in range(2):
                wide = jnp.where(mine, x[h * size:(h + 1) * size, None, :], 0.0)
                left = wide.reshape(size * some, 128).astype(jnp.bfloat16)
                got.append(jnp.dot(left, right[g, h], preferred_element_type=jnp.float32).reshape(size, some, 2 * chans))
            for o in range(2):
                to = pl.ds(o * bins + g * 2 * some, 2 * some)
                value = jnp.concatenate([got[h][:, :, o * chans:(o + 1) * chans] for h in range(2)], axis=1)
                cross[:, to, :] = value.astype(jnp.bfloat16)

        repeat(0, pairs, UNROLL, one)

    def lag(v, i):
        both = jnp.concatenate([cross[2 * i], cross[2 * i + 1]], axis=1)
        got = jnp.dot(table_ref[...], both, preferred_element_type=jnp.float32)
        if v < sends:
            both = jnp.concatenate([got[:, :chans], got[:, chans:]], axis=0)
            send[v, 2 * i * rank_of:2 * (i + 1) * rank_of] = both.astype(jnp.bfloat16)
        else:
            for r in range(2):
                out_ref[(v - sends) * size + 2 * i + r] = got[:, r * chans:(r + 1) * chans]

    def work(v):
        multiply(v)
        for i in range(size // 2):
            lag(v, i)
        if v < sends:
            exchange(v).start()

    def put(w):
        at = pl.ds(w * size, size)
        return pltpu.make_async_copy(out_ref.at[at], out_hbm.at[at], lsem.at[19 + w])

    def close(v):
        w = v - sends
        for p in range(1, peers):
            v = (p - 1) * (block // size) + w
            exchange(v).wait()
            for j in range(0, size, 2):
                value = recv[v, j * rank_of:(j + 2) * rank_of].astype(jnp.float32)
                for r in range(2):
                    at = w * size + j + r
                    out_ref[at] = out_ref[at] + value[r * rank_of:(r + 1) * rank_of]
        put(w).start()

    for c in range(chunks):
        start([core(c, 0)])
    acts = dict(core=core_in, scatter=scatter_in, side=side_in, near=functools.partial(swap_in, 0),
                next=functools.partial(swap_in, 1), gather=gather_in, back=back_in, work=work, close=close)
    for name, c in schedule(chunks, sends, kinds, halvings)[0]:
        acts[name](c)
    for w in range(block // size):
        put(w).wait()


def expand(coef_ref, basis_ref, out_ref):
    for j in range(coef_ref.shape[0]):
        value = coef_ref[j]
        high = value.astype(jnp.bfloat16)
        low = (value - high.astype(jnp.float32)).astype(jnp.bfloat16)
        both = jnp.concatenate([high, high, low], axis=0)
        out_ref[j] = lax.dot_general(both, basis_ref[...], (((0,), (0,)), ((), ())),
                                     preferred_element_type=jnp.float32)


def per_device(spectra, owners, source_rows):
    _, bins, wins, chans = spectra.shape
    steps, per_step = source_rows.shape
    n_chan, n_tm, n_freq = (lax.axis_size(a) for a in AXES[1:])
    peers = n_tm * n_freq
    per = per_step // peers
    block = steps * per
    size = min(8, block)
    chunks = steps * per_step // size
    some = 64 // wins
    pairs = bins // (2 * some)
    basis, rest = factors(bins * n_freq, 1.0 / (wins * n_tm))
    rank = basis.shape[1]
    rest = rest.reshape(rank, 2, n_freq, 2, pairs, some).transpose(2, 0, 1, 4, 3, 5).reshape(n_freq, rank, 2 * bins)
    rest = jnp.asarray(rest.astype(jnp.bfloat16))
    rest = lax.dynamic_index_in_dim(rest, lax.axis_index("freq"), 0, False) if n_freq > 1 else rest[0]
    high = basis.T.astype(np.float32).astype(jnp.bfloat16)
    low = (basis.T - high.astype(np.float64)).astype(jnp.bfloat16)
    spread = jnp.asarray(np.concatenate([high, low, high], axis=0))
    group = group_of(n_chan)
    far = max((n_chan // (2 * group)).bit_length() - 1, 1)
    sizes = (steps, per_step, bins, wins, chans, n_chan, n_tm, n_freq, size, rank)
    bf16, f32 = jnp.bfloat16, jnp.float32
    piece = (pairs // (2 * group), 2 * size, 128)
    sends = max((peers - 1) * block // size, 1)
    links = max(group - 1, 3)
    quads = max(group // 2, 1)
    dma = pltpu.SemaphoreType.DMA
    coef = pl.pallas_call(
        functools.partial(kernel, sizes),
        out_shape=jax.ShapeDtypeStruct((block, rank, chans), f32),
        in_specs=[pl.BlockSpec(memory_space=pl.ANY)] * 4,
        out_specs=pl.BlockSpec(memory_space=pl.ANY),
        scratch_shapes=[
            pltpu.VMEM((block, rank, chans), f32),
            pltpu.SMEM((steps,), jnp.int32),
            pltpu.SMEM((steps, per_step), jnp.int32),
            pltpu.VMEM((rank, 2 * bins), bf16),
            pltpu.VMEM((2, 2, bins * wins // 2, chans), bf16),
            pltpu.VMEM((steps * per_step, chans), f32),
            pltpu.VMEM((pairs, 2, 128, 2 * chans), bf16),
            pltpu.VMEM((chunks, 2, group) + piece, bf16),
            pltpu.VMEM((chunks, group) + piece, bf16),
            pltpu.VMEM((chunks, max(3 * quads, links)) + piece, bf16),
            pltpu.VMEM((chunks, far, quads) + piece, bf16),
            pltpu.VMEM((chunks, 2, group) + piece, bf16),
            pltpu.VMEM((size, 2 * bins, chans), bf16),
            pltpu.VMEM((sends, size * rank, chans), bf16),
            pltpu.VMEM((sends, size * rank, chans), bf16),
            dma((19 + block // size,)), dma((chunks, 2)), dma((chunks, 2)), dma((chunks, links)), dma((chunks, links)),
            dma((chunks, far)), dma((chunks, far)), dma((chunks, links)), dma((chunks, links)),
            dma((sends,)), dma((sends,)),
        ],
        compiler_params=pltpu.CompilerParams(collective_id=0, has_side_effects=True),
    )(owners, source_rows, spectra.reshape(2, 2, bins * wins // 2, chans), rest)
    tile = max(block // 2, 1)
    out = pl.pallas_call(
        expand,
        out_shape=jax.ShapeDtypeStruct((block, chans, LAGS), f32),
        grid=(block // tile,),
        in_specs=[pl.BlockSpec((tile, rank, chans), lambda i: (i, 0, 0)),
                  pl.BlockSpec((3 * rank, LAGS), lambda i: (0, 0))],
        out_specs=pl.BlockSpec((tile, chans, LAGS), lambda i: (i, 0, 0)),
    )(coef, spread)
    return out.reshape(steps, per, chans, LAGS)


def solution(mesh):
    placed = (P(None, "freq", "tm", ("parts", "chan")), P("parts"), P("parts", None))
    return jax.shard_map(
        per_device,
        mesh=mesh,
        in_specs=placed,
        out_specs=P(None, ("tm", "freq"), ("parts", "chan"), None),
        check_vma=False,
    )
```
